32 devices in a mesh: dp: 4 (over y, core), expert: 8 (over z, x).
Axes of the slice: x: 2, y: 2, z: 4, core: 2. Of those that a mesh axis runs over, the one named last changes fastest.
Arguments:
- hidden_in: bfloat16 [2048, 2048], P(('dp', 'expert')), may hold values from -6 to 6
- context: bfloat16 [2048, 2048], P(('dp', 'expert')), may hold values from -6 to 6
- out_proj: bfloat16 [2048, 2048], P(('dp', 'expert')), may hold values from -0.125 to 0.125
- norm_gain: float32 [2048], replicated, may hold values from 0.5 to 1.5
- router: bfloat16 [2048, 64], P(('dp', 'expert')), may hold values from -0.25 to 0.25
- expert_ids: int32 [2048, 8], P(('dp', 'expert')), may hold values from 0 to 63, as said below
- replica_expert: int32 [128], replicated, may hold values from 0 to 63, as said below
- split_pick: int32 [2048, 8], P(('dp', 'expert')), may hold values from 0 to 65535
- up_gate: bfloat16 [128, 2048, 2048], P(('dp', 'expert')), may hold values from -0.125 to 0.125
- down: bfloat16 [128, 1024, 2048], P(('dp', 'expert')), may hold values from -0.1875 to 0.1875
Outputs:
- layer_out: bfloat16 [2048, 2048], P(('dp', 'expert'))
The draws below stay inside these ranges and needn't reach their ends.
Inputs may be any that keep to these rules, and one draw needn't show every extreme that they name: `expert_ids`: each row names 8 different experts. `replica_expert`: every expert is served by one replica or more.
All inputs are finite; a program needn't handle non-finite values.
Results may differ from the reference program's by a relative error of at most 0.004.
Values may be sent and summed in bfloat16 or wider, within the bound.
A program may use at most 128 MiB of HBM per device.

```python
import jax
import jax.numpy as jnp
from jax import lax

D = 2048
FF = 1024
EXPERTS = 64
TOPK = 8
HOT = 16
TOK_DEV = 64
REPLICAS = 128
TOKENS = 2048
CAP = 8
DEVICES = 32


def expert_order(key):
    return jax.random.permutation(jax.random.fold_in(key, 101), EXPERTS).astype(jnp.int32)


def draw_replica_expert(key, part):
    order_list = expert_order(key)
    hot_list = order_list[:HOT]
    extras = hot_list[jnp.arange(REPLICAS - EXPERTS, dtype=jnp.int32) % HOT]
    listing = jnp.concatenate([jnp.arange(EXPERTS, dtype=jnp.int32), extras.astype(jnp.int32)])
    shuffle = jax.random.permutation(jax.random.fold_in(key, 102), REPLICAS)
    return listing[shuffle].astype(jnp.int32)


def draw_expert_ids(key, part):
    order_list = expert_order(key)
    hot_list = order_list[:HOT]
    cold_list = order_list[HOT:]
    hot_scores = jax.random.randint(jax.random.fold_in(key, 103), (TOKENS, HOT), 0, 1 << 20) * HOT + jnp.arange(HOT, dtype=jnp.int32)[None, :]
    cold_scores = jax.random.randint(jax.random.fold_in(key, 104), (TOKENS, EXPERTS - HOT), 0, 1 << 20) * (EXPERTS - HOT) + jnp.arange(EXPERTS - HOT, dtype=jnp.int32)[None, :]
    hot_top = lax.top_k(hot_scores, TOPK)[1]
    cold_top = lax.top_k(cold_scores, 2)[1]
    hot_ids = hot_list[hot_top]
    cold_ids = cold_list[cold_top]
    hot_number = TOPK - 2 + jax.random.randint(jax.random.fold_in(key, 105), (TOKENS, 1), 0, 2)
    column = jnp.arange(TOPK, dtype=jnp.int32)[None, :]
    cold_pick = jnp.clip(column - hot_number, 0, 1)
    from_cold = jnp.take_along_axis(cold_ids, cold_pick, axis=1)
    return jnp.where(column < hot_number, hot_ids, from_cold).astype(jnp.int32)


def set_ends(result, stream_key, low, top_value):
    longest = result.shape.index(max(result.shape))
    spots = []
    for shift in (0, 1):
        where = [jax.random.randint(jax.random.fold_in(stream_key, axis), (), 0, length) for axis, length in enumerate(result.shape)]
        where[longest] = (where[longest] + shift) % result.shape[longest]
        spots.append(tuple(where))
    return result.at[spots[0]].set(low).at[spots[1]].set(top_value)


def block_scale(own_key, extent, cuts, low, largest):
    factor_of, own = 1.0, jax.random.fold_in(own_key, 6)
    for axis_at, shards_of in cuts:
        heights = jnp.exp(jax.random.uniform(jax.random.fold_in(own, axis_at), (shards_of,), jnp.float32, low / len(cuts), largest / len(cuts)))
        factor_of = factor_of * jnp.repeat(heights, extent[axis_at] // shards_of).reshape([-1 if axis == axis_at else 1 for axis in range(len(extent))])
    return factor_of


def bell_draw(stream_key, dims, spread, most, shards=(), kind=jnp.bfloat16):
    array = spread * jax.random.normal(stream_key, dims, jnp.float32)
    if shards:
        array = array * block_scale(stream_key, dims, shards, -0.22, 0.18)
    return jnp.clip(array, -most, most).astype(kind)


def setup_inputs(seed: int = 0) -> dict:
    key_of = jax.random.split(jax.random.key(seed), 11)
    return {
        "hidden_in": bell_draw(key_of[0], (TOKENS, D), 1.0, 6.0, ((0, 32),)),
        "context": bell_draw(key_of[1], (TOKENS, D), 1.0, 6.0, ((0, 32),)),
        "out_proj": bell_draw(key_of[2], (D, D), D ** -0.5, 0.125, ((0, 32),)),
        "norm_gain": jnp.clip(1.0 + 0.1 * jax.random.normal(key_of[3], (D,), jnp.float32), 0.5, 1.5),
        "router": bell_draw(key_of[4], (D, EXPERTS), (D // 4) ** -0.5, 0.25, ((0, 32),)),
        "expert_ids": draw_expert_ids(jax.random.fold_in(key_of[10], 71), 0),
        "replica_expert": draw_replica_expert(jax.random.fold_in(key_of[10], 71), 0),
        "split_pick": set_ends(jax.random.randint(key_of[7], (TOKENS, TOPK), 0, 65536), jax.random.fold_in(key_of[7], 1), 0, 65535).astype(jnp.int32),
        "up_gate": bell_draw(key_of[8], (REPLICAS, D, 2 * FF), D ** -0.5, 0.125, ((0, 32),)),
        "down": bell_draw(key_of[9], (REPLICAS, FF, D), FF ** -0.5, 0.1875, ((0, 32),)),
    }


def rms_norm(residual, norm_gain):
    scale_back = lax.rsqrt(lax.optimization_barrier(jnp.mean(residual * residual, axis=-1, keepdims=True)) + 1e-05)
    return (residual * scale_back * norm_gain).astype(jnp.bfloat16)

def route_block(expert_ids, split_pick, replica_expert):
    replica_total = replica_expert.shape[0]
    replica_iota = lax.iota(jnp.int32, replica_total)
    same_expert = replica_expert[:, None] == replica_expert[None, :]
    earlier = replica_iota[:, None] > replica_iota[None, :]
    replica_rank = lax.optimization_barrier(jnp.sum((same_expert & earlier).astype(jnp.int32), axis=1)).astype(jnp.int32)
    serves = expert_ids[:, :, None] == replica_expert[None, None, :]
    replica_count = lax.optimization_barrier(jnp.sum(serves.astype(jnp.int32), axis=-1)).astype(jnp.int32)
    wanted = (split_pick % replica_count).astype(jnp.int32)
    matches = serves & (replica_rank[None, None, :] == wanted[:, :, None])
    replica = lax.optimization_barrier(jnp.sum(jnp.where(matches, replica_iota[None, None, :], 0), axis=-1)).astype(jnp.int32)
    flat_replica = replica.reshape(-1)
    pair_iota = lax.iota(jnp.int32, flat_replica.shape[0])
    same_target = flat_replica[:, None] == flat_replica[None, :]
    before = pair_iota[:, None] > pair_iota[None, :]
    slot_index = lax.optimization_barrier(jnp.sum((same_target & before).astype(jnp.int32), axis=1)).astype(jnp.int32)
    return (replica, slot_index.reshape(replica.shape))

def reference(hidden_in, context, out_proj, norm_gain, router, expert_ids, replica_expert, split_pick, up_gate, down):
    projected = jnp.dot(context, out_proj, preferred_element_type=jnp.float32)
    residual = hidden_in.astype(jnp.float32) + projected
    normed = rms_norm(residual, norm_gain)
    logits = jnp.dot(normed, router, preferred_element_type=jnp.float32)
    chosen = jnp.take_along_axis(logits, expert_ids, axis=1)
    raised = jnp.exp(chosen)
    route_weight = raised / lax.optimization_barrier(jnp.sum(raised, axis=-1, keepdims=True))

    def route_pair(inputs):
        return route_block(inputs[0], inputs[1], replica_expert)
    id_blocks = expert_ids.reshape(DEVICES, TOK_DEV, TOPK)
    pick_blocks = split_pick.reshape(DEVICES, TOK_DEV, TOPK)
    replica, slot_index = lax.map(route_pair, (id_blocks, pick_blocks))
    within_cap = slot_index < CAP
    source = lax.iota(jnp.int32, DEVICES)[:, None, None]
    token_index = source * TOK_DEV + lax.iota(jnp.int32, TOK_DEV)[None, :, None]
    token_index = jnp.broadcast_to(token_index, replica.shape).astype(jnp.int32)
    slot_count = DEVICES * CAP
    position = jnp.where(within_cap, replica * slot_count + source * CAP + slot_index, REPLICAS * slot_count).astype(jnp.int32)
    anchor_table = jnp.full((REPLICAS * slot_count,), -1, jnp.int32)
    anchor_table = anchor_table.at[position.reshape(-1)].set(token_index.reshape(-1), mode='drop')
    weight_table = jnp.zeros((REPLICAS * slot_count,), jnp.float32)
    weight_table = weight_table.at[position.reshape(-1)].set(route_weight.reshape(-1), mode='drop')
    anchor_table = anchor_table.reshape(REPLICAS, slot_count)
    weight_table = weight_table.reshape(REPLICAS, slot_count)

    def expert_step(summed, inputs_slice):
        anchor_row, slot_weight, replica_up, replica_down = inputs_slice
        has_row = anchor_row >= 0
        safe_index = jnp.maximum(anchor_row, 0).astype(jnp.int32)
        expert_in = jnp.where(has_row[:, None], normed[safe_index], jnp.zeros((), jnp.bfloat16))
        gate_up = jnp.dot(expert_in, replica_up, preferred_element_type=jnp.float32)
        hidden_act = (jax.nn.silu(gate_up[:, :FF]) * gate_up[:, FF:]).astype(jnp.bfloat16)
        expert_out = jnp.dot(hidden_act, replica_down, preferred_element_type=jnp.float32).astype(jnp.bfloat16)
        summed = summed.at[safe_index].add(slot_weight[:, None] * expert_out.astype(jnp.float32))
        return (summed, None)
    final = lax.scan(expert_step, residual, (anchor_table, weight_table, up_gate, down))[0]
    return final.astype(jnp.bfloat16)
```

```python
import jax
import jax.numpy as jnp
from jax import lax
from jax.sharding import PartitionSpec as P


def rms_norm(residual, norm_gain):
    scale_back = lax.rsqrt(jnp.mean(residual * residual, axis=-1, keepdims=True) + 1e-05)
    return (residual * scale_back * norm_gain).astype(jnp.bfloat16)


def route_block(expert_ids, split_pick, replica_expert):
    replica_total = replica_expert.shape[0]
    replica_iota = lax.iota(jnp.int32, replica_total)
    same_expert = replica_expert[:, None] == replica_expert[None, :]
    earlier = replica_iota[:, None] > replica_iota[None, :]
    replica_rank = jnp.sum((same_expert & earlier).astype(jnp.int32), axis=1)
    serves = expert_ids[:, :, None] == replica_expert[None, None, :]
    replica_count = jnp.sum(serves.astype(jnp.int32), axis=-1)
    wanted = split_pick % replica_count
    matches = serves & (replica_rank[None, None, :] == wanted[:, :, None])
    replica = jnp.sum(jnp.where(matches, replica_iota[None, None, :], 0), axis=-1)
    flat_replica = replica.reshape(-1)
    pair_iota = lax.iota(jnp.int32, flat_replica.shape[0])
    same_target = flat_replica[:, None] == flat_replica[None, :]
    before = pair_iota[:, None] > pair_iota[None, :]
    slot_index = jnp.sum((same_target & before).astype(jnp.int32), axis=1)
    return (replica, slot_index.reshape(replica.shape))


def apply_experts(incoming, up_gate, down, capacity):
    arrived_shape = incoming.shape
    local_reps = up_gate.shape[0]
    hidden_units = down.shape[1]
    stacked = incoming.reshape(-1, local_reps, capacity, incoming.shape[-1])
    gate_up = jnp.einsum("sjcd,jdf->sjcf", stacked, up_gate, preferred_element_type=jnp.float32)
    hidden_act = (jax.nn.silu(gate_up[..., :hidden_units]) * gate_up[..., hidden_units:]).astype(
        jnp.bfloat16
    )
    expert_out = jnp.einsum("sjcf,jfd->sjcd", hidden_act, down, preferred_element_type=jnp.float32)
    return expert_out.astype(jnp.bfloat16).reshape(arrived_shape)


def per_device(
    hidden_in,
    context,
    out_proj,
    norm_gain,
    router,
    expert_ids,
    replica_expert,
    split_pick,
    up_gate,
    down,
):
    tok_rows, model_width = hidden_in.shape
    top_count = expert_ids.shape[1]
    replica_total = replica_expert.shape[0]
    local_reps = up_gate.shape[0]
    data_groups = lax.axis_size("dp")
    expert_groups = lax.axis_size("expert")
    capacity = max(2, 2 * tok_rows * top_count // replica_total)
    summed = jnp.dot(
        context,
        lax.all_gather(out_proj, ("dp", "expert"), axis=0, tiled=True),
        preferred_element_type=jnp.float32,
    )
    router_rows = lax.all_gather(router, ("dp", "expert"), axis=0, tiled=True)
    residual = hidden_in.astype(jnp.float32) + summed
    normed = rms_norm(residual, norm_gain)
    logits = jnp.dot(normed, router_rows, preferred_element_type=jnp.float32)
    hit_mask = expert_ids[:, :, None] == lax.iota(jnp.int32, logits.shape[1])[None, None, :]
    chosen = jnp.sum(jnp.where(hit_mask, logits[:, None, :], 0.0), axis=-1)
    raised = jnp.exp(chosen)
    route_weight = raised / jnp.sum(raised, axis=-1, keepdims=True)
    replica, slot_index = route_block(expert_ids, split_pick, replica_expert)
    within_cap = slot_index < capacity
    buffer_row = jnp.where(within_cap, replica * capacity + slot_index, -1).reshape(-1)
    slot_total = replica_total * capacity
    matches = buffer_row[None, :] == lax.iota(jnp.int32, slot_total)[:, None]
    filled = jnp.any(matches, axis=1)
    row_of_pair = lax.iota(jnp.int32, tok_rows * top_count) // top_count
    anchor = jnp.sum(jnp.where(matches, row_of_pair[None, :], 0), axis=1)
    outgoing = jnp.where(filled[:, None], normed[anchor], jnp.zeros((), jnp.bfloat16))
    outgoing = outgoing.reshape(data_groups, expert_groups, local_reps * capacity, model_width)
    incoming = lax.all_to_all(
        lax.all_to_all(outgoing, "expert", split_axis=1, concat_axis=1, tiled=True),
        "dp",
        split_axis=0,
        concat_axis=0,
        tiled=True,
    )
    results = apply_experts(incoming, up_gate, down, capacity)
    returned = lax.all_to_all(
        lax.all_to_all(results, "dp", split_axis=0, concat_axis=0, tiled=True),
        "expert",
        split_axis=1,
        concat_axis=1,
        tiled=True,
    )
    returned = returned.reshape(slot_total, model_width)
    safe_index = jnp.where(within_cap, replica * capacity + slot_index, 0)
    gathered = returned[safe_index]
    kept_weight = jnp.where(within_cap, route_weight, 0.0)
    layer_out = residual + jnp.sum(kept_weight[:, :, None] * gathered.astype(jnp.float32), axis=1)
    return layer_out.astype(jnp.bfloat16)


def per_device_gathered(
    hidden_in,
    context,
    out_proj,
    norm_gain,
    router,
    expert_ids,
    replica_expert,
    split_pick,
    up_gate,
    down,
):
    axes = ("dp", "expert")
    tok_rows, model_width = hidden_in.shape
    top_count = expert_ids.shape[1]
    replica_total = replica_expert.shape[0]
    local_reps = up_gate.shape[0]
    hidden_units = down.shape[1]
    blocks = lax.axis_size("dp") * lax.axis_size("expert")
    me = lax.axis_index("dp") * lax.axis_size("expert") + lax.axis_index("expert")
    capacity = max(2, 2 * tok_rows * top_count // replica_total)
    local_slots = local_reps * capacity
    proj_rows = lax.all_gather(out_proj, axes, axis=0, tiled=True)
    router_rows = lax.all_gather(router, axes, axis=0, tiled=True)
    replica, slot_index = route_block(expert_ids, split_pick, replica_expert)
    position = jnp.where(slot_index < capacity, replica * capacity + slot_index, -1)
    positions = lax.all_gather(position, axes, axis=0, tiled=False)
    summed = jnp.dot(context, proj_rows, preferred_element_type=jnp.float32)
    residual = hidden_in.astype(jnp.float32) + summed
    normed = rms_norm(residual, norm_gain)
    all_normed = lax.all_gather(normed, axes, axis=0, tiled=False)
    logits = jnp.dot(normed, router_rows, preferred_element_type=jnp.float32)
    hit_mask = expert_ids[:, :, None] == lax.iota(jnp.int32, logits.shape[1])[None, None, :]
    chosen = jnp.sum(jnp.where(hit_mask, logits[:, None, :], 0.0), axis=-1)
    raised = jnp.exp(chosen)
    route_weight = raised / jnp.sum(raised, axis=-1, keepdims=True)
    weights = lax.all_gather(route_weight, axes, axis=0, tiled=False)
    local_iota = lax.iota(jnp.int32, local_slots)
    hits = (positions - me * local_slots)[:, :, :, None] == local_iota
    pick = jnp.any(hits, axis=2)
    slot_weight = jnp.sum(jnp.where(hits, weights[:, :, :, None], 0.0), axis=2)
    expert_in = jnp.einsum(
        "btjc,btd->jbcd",
        pick.astype(jnp.bfloat16).reshape(blocks, tok_rows, local_reps, capacity),
        all_normed,
        preferred_element_type=jnp.float32,
    ).astype(jnp.bfloat16)
    expert_in = expert_in.reshape(local_reps, blocks * capacity, model_width)
    gate_up = jnp.einsum("jsd,jdf->jsf", expert_in, up_gate, preferred_element_type=jnp.float32)
    hidden_act = (jax.nn.silu(gate_up[..., :hidden_units]) * gate_up[..., hidden_units:]).astype(
        jnp.bfloat16
    )
    expert_out = jnp.einsum("jsf,jfd->jsd", hidden_act, down, preferred_element_type=jnp.float32)
    expert_out = expert_out.astype(jnp.bfloat16).reshape(local_reps, blocks, capacity, model_width)
    upper = slot_weight.astype(jnp.bfloat16)
    lower = (slot_weight - upper.astype(jnp.float32)).astype(jnp.bfloat16)
    split = jnp.stack([upper, lower]).reshape(2, blocks, tok_rows, local_reps, capacity)
    twice = jnp.broadcast_to(expert_out[None], (2,) + expert_out.shape)
    partial = jnp.einsum(
        "hbtjc,hjbcd->btd", split, twice, preferred_element_type=jnp.float32
    ).astype(jnp.bfloat16)
    combined = lax.psum_scatter(partial, axes, scatter_dimension=0, tiled=False)
    return (residual + combined.astype(jnp.float32)).astype(jnp.bfloat16)


def solution(mesh):
    device_count = mesh.shape["dp"] * mesh.shape["expert"]
    plan = per_device_gathered if device_count <= 32 else per_device
    return jax.shard_map(
        plan,
        mesh=mesh,
        in_specs=(
            P(("dp", "expert"), None),
            P(("dp", "expert"), None),
            P(("dp", "expert"), None),
            P(),
            P(("dp", "expert"), None),
            P(("dp", "expert"), None),
            P(),
            P(("dp", "expert"), None),
            P(("dp", "expert"), None, None),
            P(("dp", "expert"), None, None),
        ),
        out_specs=P(("dp", "expert"), None),
        check_vma=False,
    )
```

```python
import functools

import jax
import jax.numpy as jnp
from jax import lax
from jax.experimental import pallas as pl
from jax.experimental.pallas import tpu as pltpu
from jax.sharding import PartitionSpec as P


def rms_norm(residual, norm_gain):
    scale_back = lax.rsqrt(jnp.mean(residual * residual, axis=-1, keepdims=True) + 1e-05)
    return (residual * scale_back * norm_gain).astype(jnp.bfloat16)


def route_block(expert_ids, split_pick, replica_expert):
    replica_total = replica_expert.shape[0]
    replica_iota = lax.iota(jnp.int32, replica_total)
    same_expert = replica_expert[:, None] == replica_expert[None, :]
    earlier = replica_iota[:, None] > replica_iota[None, :]
    replica_rank = jnp.sum((same_expert & earlier).astype(jnp.int32), axis=1)
    serves = expert_ids[:, :, None] == replica_expert[None, None, :]
    replica_count = jnp.sum(serves.astype(jnp.int32), axis=-1)
    wanted = split_pick % replica_count
    matches = serves & (replica_rank[None, None, :] == wanted[:, :, None])
    replica = jnp.sum(jnp.where(matches, replica_iota[None, None, :], 0), axis=-1)
    flat_replica = replica.reshape(-1)
    pair_iota = lax.iota(jnp.int32, flat_replica.shape[0])
    same_target = flat_replica[:, None] == flat_replica[None, :]
    before = pair_iota[:, None] > pair_iota[None, :]
    slot_index = jnp.sum((same_target & before).astype(jnp.int32), axis=1)
    return (replica, slot_index.reshape(replica.shape))


def apply_experts(incoming, up_gate, down, capacity):
    arrived_shape = incoming.shape
    local_reps = up_gate.shape[0]
    hidden_units = down.shape[1]
    stacked = incoming.reshape(-1, local_reps, capacity, incoming.shape[-1])
    gate_up = jnp.einsum("sjcd,jdf->sjcf", stacked, up_gate, preferred_element_type=jnp.float32)
    hidden_act = (jax.nn.silu(gate_up[..., :hidden_units]) * gate_up[..., hidden_units:]).astype(
        jnp.bfloat16
    )
    expert_out = jnp.einsum("sjcf,jfd->sjcd", hidden_act, down, preferred_element_type=jnp.float32)
    return expert_out.astype(jnp.bfloat16).reshape(arrived_shape)


def per_device(
    hidden_in,
    context,
    out_proj,
    norm_gain,
    router,
    expert_ids,
    replica_expert,
    split_pick,
    up_gate,
    down,
):
    tok_rows, model_width = hidden_in.shape
    top_count = expert_ids.shape[1]
    replica_total = replica_expert.shape[0]
    local_reps = up_gate.shape[0]
    data_groups = lax.axis_size("dp")
    expert_groups = lax.axis_size("expert")
    capacity = max(2, 2 * tok_rows * top_count // replica_total)
    summed = jnp.dot(
        context,
        lax.all_gather(out_proj, ("dp", "expert"), axis=0, tiled=True),
        preferred_element_type=jnp.float32,
    )
    router_rows = lax.all_gather(router, ("dp", "expert"), axis=0, tiled=True)
    residual = hidden_in.astype(jnp.float32) + summed
    normed = rms_norm(residual, norm_gain)
    logits = jnp.dot(normed, router_rows, preferred_element_type=jnp.float32)
    hit_mask = expert_ids[:, :, None] == lax.iota(jnp.int32, logits.shape[1])[None, None, :]
    chosen = jnp.sum(jnp.where(hit_mask, logits[:, None, :], 0.0), axis=-1)
    raised = jnp.exp(chosen)
    route_weight = raised / jnp.sum(raised, axis=-1, keepdims=True)
    replica, slot_index = route_block(expert_ids, split_pick, replica_expert)
    within_cap = slot_index < capacity
    buffer_row = jnp.where(within_cap, replica * capacity + slot_index, -1).reshape(-1)
    slot_total = replica_total * capacity
    matches = buffer_row[None, :] == lax.iota(jnp.int32, slot_total)[:, None]
    filled = jnp.any(matches, axis=1)
    row_of_pair = lax.iota(jnp.int32, tok_rows * top_count) // top_count
    anchor = jnp.sum(jnp.where(matches, row_of_pair[None, :], 0), axis=1)
    outgoing = jnp.where(filled[:, None], normed[anchor], jnp.zeros((), jnp.bfloat16))
    outgoing = outgoing.reshape(data_groups, expert_groups, local_reps * capacity, model_width)
    incoming = lax.all_to_all(
        lax.all_to_all(outgoing, "expert", split_axis=1, concat_axis=1, tiled=True),
        "dp",
        split_axis=0,
        concat_axis=0,
        tiled=True,
    )
    results = apply_experts(incoming, up_gate, down, capacity)
    returned = lax.all_to_all(
        lax.all_to_all(results, "dp", split_axis=0, concat_axis=0, tiled=True),
        "expert",
        split_axis=1,
        concat_axis=1,
        tiled=True,
    )
    returned = returned.reshape(slot_total, model_width)
    safe_index = jnp.where(within_cap, replica * capacity + slot_index, 0)
    gathered = returned[safe_index]
    kept_weight = jnp.where(within_cap, route_weight, 0.0)
    layer_out = residual + jnp.sum(kept_weight[:, :, None] * gathered.astype(jnp.float32), axis=1)
    return layer_out.astype(jnp.bfloat16)

MESH = pl.DeviceIdType.MESH


def place():
    d, e = lax.axis_index("dp"), lax.axis_index("expert")
    return d // 2, d % 2, e // 2, e % 2


def device_of(y, c, z, x):
    return (y * 2 + c, z * 2 + x)


def block_of(y, c, z, x):
    return (y * 2 + c) * (2 * LINE) + z * 2 + x


LINE = 4


def greet(barrier, y, c, z, x):
    for other in (device_of(y, 1 - c, z, x), device_of(1 - y, c, z, x), device_of(y, c, z, 1 - x)):
        pl.semaphore_signal(barrier, inc=1, device_id=other, device_id_type=MESH)

    @pl.when(z > 0)
    def _():
        pl.semaphore_signal(barrier, inc=1, device_id=device_of(y, c, z - 1, x), device_id_type=MESH)

    @pl.when(z < LINE - 1)
    def _():
        pl.semaphore_signal(barrier, inc=1, device_id=device_of(y, c, z + 1, x), device_id_type=MESH)

    pl.semaphore_wait(barrier, 3 + jnp.minimum(z, 1) + jnp.minimum(LINE - 1 - z, 1))


def gather_kernel(half, in_ref, out_ref, own_sem, line_sem, x_sem, y_sem, core_sem, recv_sem):
    y, c, z, x = place()
    greet(pltpu.get_barrier_semaphore(), y, c, z, x)
    me = block_of(y, c, z, x)
    up, down = device_of(y, c, z + 1, x), device_of(y, c, z - 1, x)
    over_x, over_y = device_of(y, c, z, 1 - x), device_of(1 - y, c, z, x)
    twin = device_of(y, 1 - c, z, x)

    def piece(block, h):
        return out_ref.at[block, pl.ds(h * half, half)]

    def send(block, h, target, sem, own=False):
        return pltpu.make_async_remote_copy(
            src_ref=in_ref.at[pl.ds(h * half, half)] if own else piece(block, h),
            dst_ref=piece(block, h),
            send_sem=sem,
            recv_sem=recv_sem.at[block, h],
            device_id=target,
            device_id_type=MESH,
        )

    def arrive(block, h):
        send(block, h, twin, core_sem.at[0, 0]).wait_recv()

    local = pltpu.make_async_copy(in_ref, out_ref.at[me], own_sem)
    local.start()

    def spread(source_z, own, going, act):
        block = block_of(y, c, source_z, x)
        for h in range(2):
            if going >= 0:
                @pl.when(z < LINE - 1)
                def _():
                    act(send(block, h, up, line_sem.at[0, source_z, h], own))
            if going <= 0:
                @pl.when(z > 0)
                def _():
                    act(send(block, h, down, line_sem.at[1, source_z, h], own))
        for h in range(2):
            act(send(block, h, over_x, x_sem.at[source_z, h], own))
            act(send(block, 1 - h, over_y, y_sem.at[source_z, 1 - h], own))
        for h in range(2):
            act(send(block, h, twin, core_sem.at[source_z, h], own))

    def hand_on(source_z, act, wait):
        from_x = block_of(y, c, source_z, 1 - x)
        from_y = block_of(1 - y, c, source_z, x)
        if wait:
            arrive(from_x, 0)
        act(send(from_x, 0, over_y, y_sem.at[source_z, 2]))
        act(send(from_x, 0, twin, core_sem.at[LINE + source_z, 0]))
        if wait:
            arrive(from_y, 1)
        act(send(from_y, 1, over_x, x_sem.at[source_z, 2]))
        act(send(from_y, 1, twin, core_sem.at[2 * LINE + source_z, 1]))
        if wait:
            arrive(from_x, 1)
        act(send(from_x, 1, twin, core_sem.at[LINE + source_z, 1]))
        if wait:
            arrive(from_y, 0)
        act(send(from_y, 0, twin, core_sem.at[2 * LINE + source_z, 0]))

    def last_leg(source_z, act, wait):
        across = block_of(1 - y, c, source_z, 1 - x)
        for h in range(2):
            if wait:
                arrive(across, h)
            act(send(across, h, twin, core_sem.at[3 * LINE + source_z, h]))

    def start(copy):
        copy.start()

    def drain(copy):
        copy.wait_send()

    def by_distance(k, step):
        @pl.when(z >= k)
        def _():
            step(z - k, 1)

        @pl.when(z + k < LINE)
        def _():
            step(z + k, -1)

    def come_along_z(source_z, going):
        for h in range(2):
            arrive(block_of(y, c, source_z, x), h)
        spread(source_z, False, going, start)

    spread(z, True, 0, start)
    by_distance(1, come_along_z)
    hand_on(z, start, True)
    by_distance(2, come_along_z)
    by_distance(1, lambda source_z, going: hand_on(source_z, start, True))
    by_distance(3, come_along_z)
    last_leg(z, start, True)
    by_distance(2, lambda source_z, going: hand_on(source_z, start, True))
    by_distance(1, lambda source_z, going: last_leg(source_z, start, True))
    by_distance(3, lambda source_z, going: hand_on(source_z, start, True))
    by_distance(2, lambda source_z, going: last_leg(source_z, start, True))
    by_distance(3, lambda source_z, going: last_leg(source_z, start, True))
    for other_y in range(2):
        for other_x in range(2):
            for source_z in range(LINE):
                for h in range(2):
                    arrive(block_of(other_y, 1 - c, source_z, other_x), h)
    spread(z, True, 0, drain)
    for k in range(1, LINE):
        by_distance(k, lambda source_z, going: spread(source_z, False, going, drain))
    for source_z in range(LINE):
        hand_on(source_z, drain, False)
        last_leg(source_z, drain, False)
    local.wait()


def gather_rows(array, collective_id):
    rows, width = array.shape
    blocks = 8 * LINE
    dma = pltpu.SemaphoreType.DMA
    return pl.pallas_call(
        functools.partial(gather_kernel, rows // 2),
        out_shape=jax.ShapeDtypeStruct((blocks, rows, width), array.dtype),
        in_specs=[pl.BlockSpec(memory_space=pl.ANY)],
        out_specs=pl.BlockSpec(memory_space=pl.ANY),
        scratch_shapes=[
            dma,
            dma((2, LINE, 2)),
            dma((LINE, 3)),
            dma((LINE, 3)),
            dma((4 * LINE, 2)),
            dma((blocks, 2)),
        ],
        compiler_params=pltpu.CompilerParams(collective_id=collective_id, has_side_effects=True),
    )(array)


def scatter_kernel(half, in_ref, out_ref, core_buf, x_buf, y_buf, diag_buf, line_buf, core_sem, x_sem, y_sem,
                   line_sem, core_recv, x_recv, y_recv, diag_recv, line_recv):
    y, c, z, x = place()
    greet(pltpu.get_barrier_semaphore(), y, c, z, x)
    up, down = device_of(y, c, z + 1, x), device_of(y, c, z - 1, x)
    over_x, over_y = device_of(y, c, z, 1 - x), device_of(1 - y, c, z, x)
    twin = device_of(y, 1 - c, z, x)

    def block(quadrant, target_z, core):
        return block_of(*((1 - y) if quadrant >= 2 else y, core, target_z, (1 - x) if quadrant % 2 else x))

    def part(h):
        return pl.ds(h * half, half)

    def remote(src, dst, send_sem, recv_sem, target):
        return pltpu.make_async_remote_copy(
            src_ref=src, dst_ref=dst, send_sem=send_sem, recv_sem=recv_sem, device_id=target, device_id_type=MESH
        )

    def to_core(q, tz, h):
        return remote(
            in_ref.at[block(q, tz, 1 - c), part(h)],
            core_buf.at[q, tz, part(h)],
            core_sem.at[q, tz, h],
            core_recv.at[q, tz, h],
            twin,
        )

    def across(tz, h):
        return remote(
            core_buf.at[3, tz, part(h)],
            diag_buf.at[h, tz],
            (y_sem if h == 0 else x_sem).at[tz, 2],
            diag_recv.at[h, tz],
            over_y if h == 0 else over_x,
        )

    def to_x(tz, h):
        return remote(core_buf.at[1, tz, part(h)], x_buf.at[tz, part(h)], x_sem.at[tz, h], x_recv.at[tz, h], over_x)

    def to_y(tz, h):
        return remote(core_buf.at[2, tz, part(h)], y_buf.at[tz, part(h)], y_sem.at[tz, h], y_recv.at[tz, h], over_y)

    def along(way, tz):
        return remote(
            core_buf.at[0, tz], line_buf.at[way, tz], line_sem.at[way, tz], line_recv.at[way, tz],
            up if way == 0 else down,
        )

    def add_into(target, source):
        target[...] = (target[...].astype(jnp.float32) + source[...].astype(jnp.float32)).astype(target.dtype)

    def add_core(q, tz, h):
        to_core(q, tz, h).wait_recv()
        add_into(core_buf.at[q, tz, part(h)], in_ref.at[block(q, tz, c), part(h)])

    def through(tz):
        for h in range(2):
            add_core(3, tz, h)
            across(tz, h).start()
        add_core(1, tz, 1)
        to_x(tz, 1).start()
        add_core(2, tz, 0)
        to_y(tz, 0).start()
        add_core(1, tz, 0)
        across(tz, 0).wait_recv()
        add_into(core_buf.at[1, tz, part(0)], diag_buf.at[0, tz])
        to_x(tz, 0).start()
        add_core(2, tz, 1)
        across(tz, 1).wait_recv()
        add_into(core_buf.at[2, tz, part(1)], diag_buf.at[1, tz])
        to_y(tz, 1).start()
        for h in range(2):
            add_core(0, tz, h)

    def collect(tz):
        for h in (1, 0):
            to_x(tz, h).wait_recv()
            add_into(core_buf.at[0, tz, part(h)], x_buf.at[tz, part(h)])
        for h in (0, 1):
            to_y(tz, h).wait_recv()
            add_into(core_buf.at[0, tz, part(h)], y_buf.at[tz, part(h)])

    def by_distance(k, step):
        @pl.when(z + k < LINE)
        def _():
            step(z + k, 0)

        @pl.when(z >= k)
        def _():
            step(z - k, 1)

    def pass_on(tz, way):
        collect(tz)

        @pl.when((z > 0) if way == 0 else (z < LINE - 1))
        def _():
            along(way, tz).wait_recv()
            add_into(core_buf.at[0, tz], line_buf.at[way, tz])

        along(way, tz).start()

    for k in (3, 2, 1, 0):
        def offer(tz, way):
            for q in (3, 1, 2, 0):
                for h in ((1, 0) if q == 1 else (0, 1)):
                    to_core(q, tz, h).start()

        if k:
            by_distance(k, offer)
        else:
            offer(z, 0)
    by_distance(3, lambda tz, way: through(tz))
    by_distance(2, lambda tz, way: through(tz))
    by_distance(3, pass_on)
    by_distance(1, lambda tz, way: through(tz))
    by_distance(2, pass_on)
    through(z)
    by_distance(1, pass_on)
    collect(z)

    @pl.when(z > 0)
    def _():
        along(0, z).wait_recv()
        add_into(core_buf.at[0, z], line_buf.at[0, z])

    @pl.when(z < LINE - 1)
    def _():
        along(1, z).wait_recv()
        add_into(core_buf.at[0, z], line_buf.at[1, z])

    out_ref[...] = core_buf[0, z]
    for tz in range(LINE):
        for q in range(4):
            for h in range(2):
                to_core(q, tz, h).wait_send()
        for h in range(2):
            across(tz, h).wait_send()
            to_x(tz, h).wait_send()
            to_y(tz, h).wait_send()
    for k in (1, 2, 3):
        by_distance(k, lambda tz, way: along(way, tz).wait_send())


def scatter_sum(partial, collective_id):
    blocks, rows, width = partial.shape
    half = rows // 2
    dma = pltpu.SemaphoreType.DMA
    return pl.pallas_call(
        functools.partial(scatter_kernel, half),
        out_shape=jax.ShapeDtypeStruct((rows, width), partial.dtype),
        in_specs=[pl.BlockSpec(memory_space=pltpu.VMEM)],
        out_specs=pl.BlockSpec(memory_space=pltpu.VMEM),
        scratch_shapes=[
            pltpu.VMEM((4, LINE, rows, width), partial.dtype),
            pltpu.VMEM((LINE, rows, width), partial.dtype),
            pltpu.VMEM((LINE, rows, width), partial.dtype),
            pltpu.VMEM((2, LINE, half, width), partial.dtype),
            pltpu.VMEM((2, LINE, rows, width), partial.dtype),
            dma((4, LINE, 2)),
            dma((LINE, 3)),
            dma((LINE, 3)),
            dma((2, LINE)),
            dma((4, LINE, 2)),
            dma((LINE, 2)),
            dma((LINE, 2)),
            dma((2, LINE)),
            dma((2, LINE)),
        ],
        compiler_params=pltpu.CompilerParams(
            collective_id=collective_id, has_side_effects=True, vmem_limit_bytes=48 << 20
        ),
    )(partial)


SIDE = 128


def per_device_gathered(
    hidden_in,
    context,
    out_proj,
    norm_gain,
    router,
    expert_ids,
    replica_expert,
    split_pick,
    up_gate,
    down,
):
    tok_rows, model_width = hidden_in.shape
    expert_total = router.shape[1]
    top_count = expert_ids.shape[1]
    replica_total = replica_expert.shape[0]
    local_reps = up_gate.shape[0]
    hidden_units = down.shape[1]
    blocks = lax.axis_size("dp") * lax.axis_size("expert")
    me = lax.axis_index("dp") * lax.axis_size("expert") + lax.axis_index("expert")
    capacity = max(2, 2 * tok_rows * top_count // replica_total)
    local_slots = local_reps * capacity
    side = jnp.pad(router, ((0, 0), (0, SIDE - expert_total)))
    proj_rows = gather_rows(jnp.concatenate([out_proj, side], axis=1), 0)
    proj_rows = proj_rows.reshape(blocks * out_proj.shape[0], model_width + SIDE)
    router_rows = proj_rows[:, model_width : model_width + expert_total]
    replica, slot_index = route_block(expert_ids, split_pick, replica_expert)
    slot_index = jnp.minimum(slot_index, capacity)
    summed = jnp.dot(context, proj_rows, preferred_element_type=jnp.float32)[:, :model_width]
    residual = hidden_in.astype(jnp.float32) + summed
    normed = rms_norm(residual, norm_gain)
    logits = jnp.dot(normed, router_rows, preferred_element_type=jnp.float32)
    hit_mask = expert_ids[:, :, None] == lax.iota(jnp.int32, expert_total)[None, None, :]
    chosen = jnp.sum(jnp.where(hit_mask, logits[:, None, :], 0.0), axis=-1)
    raised = jnp.exp(chosen)
    route_weight = raised / jnp.sum(raised, axis=-1, keepdims=True)
    upper = route_weight.astype(jnp.bfloat16)
    lower = (route_weight - upper.astype(jnp.float32)).astype(jnp.bfloat16)
    side = jnp.concatenate(
        [upper, lower, replica.astype(jnp.bfloat16), slot_index.astype(jnp.bfloat16)], axis=1
    )
    side = jnp.pad(side, ((0, 0), (0, SIDE - 4 * top_count)))
    all_rows = gather_rows(jnp.concatenate([normed, side], axis=1), 1)
    side = all_rows[:, :, model_width : model_width + 4 * top_count]
    upper, lower, replica, slot_index = [
        side[:, :, part * top_count : (part + 1) * top_count] for part in range(4)
    ]
    replica = replica.astype(jnp.int32) - me * local_reps
    slot_index = slot_index.astype(jnp.int32)
    place_here = jnp.where(slot_index < capacity, replica * capacity + slot_index, -1)
    hits = place_here[:, :, :, None] == lax.iota(jnp.int32, local_slots)
    pick = jnp.any(hits, axis=2).astype(jnp.bfloat16)
    upper = jnp.sum(jnp.where(hits, upper[:, :, :, None], 0), axis=2)
    lower = jnp.sum(jnp.where(hits, lower[:, :, :, None], 0), axis=2)
    expert_in = jnp.einsum(
        "btjc,btd->jbcd",
        pick.reshape(blocks, tok_rows, local_reps, capacity),
        all_rows,
        preferred_element_type=jnp.float32,
    ).astype(jnp.bfloat16)
    expert_in = expert_in[..., :model_width].reshape(local_reps, blocks * capacity, model_width)
    gate_up = jnp.einsum("jsd,jdf->jsf", expert_in, up_gate, preferred_element_type=jnp.float32)
    hidden_act = (jax.nn.silu(gate_up[..., :hidden_units]) * gate_up[..., hidden_units:]).astype(
        jnp.bfloat16
    )
    expert_out = jnp.einsum("jsf,jfd->jsd", hidden_act, down, preferred_element_type=jnp.float32)
    expert_out = expert_out.astype(jnp.bfloat16).reshape(local_reps, blocks, capacity, model_width)
    split = jnp.stack([upper, lower]).reshape(2, blocks, tok_rows, local_reps, capacity)
    twice = jnp.broadcast_to(expert_out[None], (2,) + expert_out.shape)
    partial = jnp.einsum(
        "hbtjc,hjbcd->btd", split, twice, preferred_element_type=jnp.float32
    ).astype(jnp.bfloat16)
    combined = scatter_sum(partial, 2)
    return (residual + combined.astype(jnp.float32)).astype(jnp.bfloat16)


def solution(mesh):
    plan = per_device_gathered if (mesh.shape["dp"], mesh.shape["expert"]) == (4, 8) else per_device
    return jax.shard_map(
        plan,
        mesh=mesh,
        in_specs=(
            P(("dp", "expert"), None),
            P(("dp", "expert"), None),
            P(("dp", "expert"), None),
            P(),
            P(("dp", "expert"), None),
            P(("dp", "expert"), None),
            P(),
            P(("dp", "expert"), None),
            P(("dp", "expert"), None, None),
            P(("dp", "expert"), None, None),
        ),
        out_specs=P(("dp", "expert"), None),
        check_vma=False,
    )
```

```python
import functools

import jax
import jax.numpy as jnp
from jax import lax
from jax.experimental import pallas as pl
from jax.experimental.pallas import tpu as pltpu
from jax.sharding import PartitionSpec as P


def rms_norm(residual, norm_gain):
    scale_back = lax.rsqrt(jnp.mean(residual * residual, axis=-1, keepdims=True) + 1e-05)
    return (residual * scale_back * norm_gain).astype(jnp.bfloat16)


def route_block(expert_ids, split_pick, replica_expert):
    replica_total = replica_expert.shape[0]
    replica_iota = lax.iota(jnp.int32, replica_total)
    same_expert = replica_expert[:, None] == replica_expert[None, :]
    earlier = replica_iota[:, None] > replica_iota[None, :]
    replica_rank = jnp.sum((same_expert & earlier).astype(jnp.int32), axis=1)
    serves = expert_ids[:, :, None] == replica_expert[None, None, :]
    replica_count = jnp.sum(serves.astype(jnp.int32), axis=-1)
    wanted = split_pick % replica_count
    matches = serves & (replica_rank[None, None, :] == wanted[:, :, None])
    replica = jnp.sum(jnp.where(matches, replica_iota[None, None, :], 0), axis=-1)
    flat_replica = replica.reshape(-1)
    pair_iota = lax.iota(jnp.int32, flat_replica.shape[0])
    same_target = flat_replica[:, None] == flat_replica[None, :]
    before = pair_iota[:, None] > pair_iota[None, :]
    slot_index = jnp.sum((same_target & before).astype(jnp.int32), axis=1)
    return (replica, slot_index.reshape(replica.shape))


def apply_experts(incoming, up_gate, down, capacity):
    arrived_shape = incoming.shape
    local_reps = up_gate.shape[0]
    hidden_units = down.shape[1]
    stacked = incoming.reshape(-1, local_reps, capacity, incoming.shape[-1])
    gate_up = jnp.einsum("sjcd,jdf->sjcf", stacked, up_gate, preferred_element_type=jnp.float32)
    hidden_act = (jax.nn.silu(gate_up[..., :hidden_units]) * gate_up[..., hidden_units:]).astype(
        jnp.bfloat16
    )
    expert_out = jnp.einsum("sjcf,jfd->sjcd", hidden_act, down, preferred_element_type=jnp.float32)
    return expert_out.astype(jnp.bfloat16).reshape(arrived_shape)


def per_device(
    hidden_in,
    context,
    out_proj,
    norm_gain,
    router,
    expert_ids,
    replica_expert,
    split_pick,
    up_gate,
    down,
):
    tok_rows, model_width = hidden_in.shape
    top_count = expert_ids.shape[1]
    replica_total = replica_expert.shape[0]
    local_reps = up_gate.shape[0]
    data_groups = lax.axis_size("dp")
    expert_groups = lax.axis_size("expert")
    capacity = max(2, 2 * tok_rows * top_count // replica_total)
    summed = jnp.dot(
        context,
        lax.all_gather(out_proj, ("dp", "expert"), axis=0, tiled=True),
        preferred_element_type=jnp.float32,
    )
    router_rows = lax.all_gather(router, ("dp", "expert"), axis=0, tiled=True)
    residual = hidden_in.astype(jnp.float32) + summed
    normed = rms_norm(residual, norm_gain)
    logits = jnp.dot(normed, router_rows, preferred_element_type=jnp.float32)
    hit_mask = expert_ids[:, :, None] == lax.iota(jnp.int32, logits.shape[1])[None, None, :]
    chosen = jnp.sum(jnp.where(hit_mask, logits[:, None, :], 0.0), axis=-1)
    raised = jnp.exp(chosen)
    route_weight = raised / jnp.sum(raised, axis=-1, keepdims=True)
    replica, slot_index = route_block(expert_ids, split_pick, replica_expert)
    within_cap = slot_index < capacity
    buffer_row = jnp.where(within_cap, replica * capacity + slot_index, -1).reshape(-1)
    slot_total = replica_total * capacity
    matches = buffer_row[None, :] == lax.iota(jnp.int32, slot_total)[:, None]
    filled = jnp.any(matches, axis=1)
    row_of_pair = lax.iota(jnp.int32, tok_rows * top_count) // top_count
    anchor = jnp.sum(jnp.where(matches, row_of_pair[None, :], 0), axis=1)
    outgoing = jnp.where(filled[:, None], normed[anchor], jnp.zeros((), jnp.bfloat16))
    outgoing = outgoing.reshape(data_groups, expert_groups, local_reps * capacity, model_width)
    incoming = lax.all_to_all(
        lax.all_to_all(outgoing, "expert", split_axis=1, concat_axis=1, tiled=True),
        "dp",
        split_axis=0,
        concat_axis=0,
        tiled=True,
    )
    results = apply_experts(incoming, up_gate, down, capacity)
    returned = lax.all_to_all(
        lax.all_to_all(results, "dp", split_axis=0, concat_axis=0, tiled=True),
        "expert",
        split_axis=1,
        concat_axis=1,
        tiled=True,
    )
    returned = returned.reshape(slot_total, model_width)
    safe_index = jnp.where(within_cap, replica * capacity + slot_index, 0)
    gathered = returned[safe_index]
    kept_weight = jnp.where(within_cap, route_weight, 0.0)
    layer_out = residual + jnp.sum(kept_weight[:, :, None] * gathered.astype(jnp.float32), axis=1)
    return layer_out.astype(jnp.bfloat16)

MESH = pl.DeviceIdType.MESH


def place():
    d, e = lax.axis_index("dp"), lax.axis_index("expert")
    return d // 2, d % 2, e // 2, e % 2


def device_of(y, c, z, x):
    return (y * 2 + c, z * 2 + x)


def block_of(y, c, z, x):
    return (y * 2 + c) * (2 * LINE) + z * 2 + x


LINE = 4


def greet(barrier, y, c, z, x):
    for other in (device_of(y, 1 - c, z, x), device_of(1 - y, c, z, x), device_of(y, c, z, 1 - x)):
        pl.semaphore_signal(barrier, inc=1, device_id=other, device_id_type=MESH)

    @pl.when(z > 0)
    def _():
        pl.semaphore_signal(barrier, inc=1, device_id=device_of(y, c, z - 1, x), device_id_type=MESH)

    @pl.when(z < LINE - 1)
    def _():
        pl.semaphore_signal(barrier, inc=1, device_id=device_of(y, c, z + 1, x), device_id_type=MESH)

    pl.semaphore_wait(barrier, 3 + jnp.minimum(z, 1) + jnp.minimum(LINE - 1 - z, 1))


def gather_kernel(half, in_ref, out_ref, own_sem, line_sem, x_sem, y_sem, core_sem, recv_sem):
    y, c, z, x = place()
    greet(pltpu.get_barrier_semaphore(), y, c, z, x)
    me = block_of(y, c, z, x)
    up, down = device_of(y, c, z + 1, x), device_of(y, c, z - 1, x)
    over_x, over_y = device_of(y, c, z, 1 - x), device_of(1 - y, c, z, x)
    twin = device_of(y, 1 - c, z, x)

    def piece(block, h):
        return out_ref.at[block, pl.ds(h * half, half)]

    def send(block, h, target, sem, own=False):
        return pltpu.make_async_remote_copy(
            src_ref=in_ref.at[pl.ds(h * half, half)] if own else piece(block, h),
            dst_ref=piece(block, h),
            send_sem=sem,
            recv_sem=recv_sem.at[block, h],
            device_id=target,
            device_id_type=MESH,
        )

    def arrive(block, h):
        send(block, h, twin, core_sem.at[0, 0]).wait_recv()

    local = pltpu.make_async_copy(in_ref, out_ref.at[me], own_sem)
    local.start()

    def spread(source_z, own, going, act):
        block = block_of(y, c, source_z, x)
        for h in range(2):
            if going >= 0:
                @pl.when(z < LINE - 1)
                def _():
                    act(send(block, h, up, line_sem.at[0, source_z, h], own))
            if going <= 0:
                @pl.when(z > 0)
                def _():
                    act(send(block, h, down, line_sem.at[1, source_z, h], own))
        for h in range(2):
            act(send(block, h, over_x, x_sem.at[source_z, h], own))
            act(send(block, 1 - h, over_y, y_sem.at[source_z, 1 - h], own))
        for h in range(2):
            act(send(block, h, twin, core_sem.at[source_z, h], own))

    def hand_on(source_z, act, wait):
        from_x = block_of(y, c, source_z, 1 - x)
        from_y = block_of(1 - y, c, source_z, x)
        if wait:
            arrive(from_x, 0)
        act(send(from_x, 0, over_y, y_sem.at[source_z, 2]))
        act(send(from_x, 0, twin, core_sem.at[LINE + source_z, 0]))
        if wait:
            arrive(from_y, 1)
        act(send(from_y, 1, over_x, x_sem.at[source_z, 2]))
        act(send(from_y, 1, twin, core_sem.at[2 * LINE + source_z, 1]))
        if wait:
            arrive(from_x, 1)
        act(send(from_x, 1, twin, core_sem.at[LINE + source_z, 1]))
        if wait:
            arrive(from_y, 0)
        act(send(from_y, 0, twin, core_sem.at[2 * LINE + source_z, 0]))

    def last_leg(source_z, act, wait):
        across = block_of(1 - y, c, source_z, 1 - x)
        for h in range(2):
            if wait:
                arrive(across, h)
            act(send(across, h, twin, core_sem.at[3 * LINE + source_z, h]))

    def start(copy):
        copy.start()

    def drain(copy):
        copy.wait_send()

    def by_distance(k, step):
        @pl.when(z >= k)
        def _():
            step(z - k, 1)

        @pl.when(z + k < LINE)
        def _():
            step(z + k, -1)

    def come_along_z(source_z, going):
        for h in range(2):
            arrive(block_of(y, c, source_z, x), h)
        spread(source_z, False, going, start)

    spread(z, True, 0, start)
    by_distance(1, come_along_z)
    hand_on(z, start, True)
    by_distance(2, come_along_z)
    by_distance(1, lambda source_z, going: hand_on(source_z, start, True))
    by_distance(3, come_along_z)
    last_leg(z, start, True)
    by_distance(2, lambda source_z, going: hand_on(source_z, start, True))
    by_distance(1, lambda source_z, going: last_leg(source_z, start, True))
    by_distance(3, lambda source_z, going: hand_on(source_z, start, True))
    by_distance(2, lambda source_z, going: last_leg(source_z, start, True))
    by_distance(3, lambda source_z, going: last_leg(source_z, start, True))
    for other_y in range(2):
        for other_x in range(2):
            for source_z in range(LINE):
                for h in range(2):
                    arrive(block_of(other_y, 1 - c, source_z, other_x), h)
    spread(z, True, 0, drain)
    for k in range(1, LINE):
        by_distance(k, lambda source_z, going: spread(source_z, False, going, drain))
    for source_z in range(LINE):
        hand_on(source_z, drain, False)
        last_leg(source_z, drain, False)
    local.wait()


def gather_rows(array, collective_id):
    rows, width = array.shape
    blocks = 8 * LINE
    dma = pltpu.SemaphoreType.DMA
    return pl.pallas_call(
        functools.partial(gather_kernel, rows // 2),
        out_shape=jax.ShapeDtypeStruct((blocks, rows, width), array.dtype),
        in_specs=[pl.BlockSpec(memory_space=pl.ANY)],
        out_specs=pl.BlockSpec(memory_space=pl.ANY),
        scratch_shapes=[
            dma,
            dma((2, LINE, 2)),
            dma((LINE, 3)),
            dma((LINE, 3)),
            dma((4 * LINE, 2)),
            dma((blocks, 2)),
        ],
        compiler_params=pltpu.CompilerParams(collective_id=collective_id, has_side_effects=True),
    )(array)


def scatter_kernel(half, in_ref, out_ref, core_buf, x_buf, y_buf, diag_buf, line_buf, core_sem, x_sem, y_sem,
                   line_sem, core_recv, x_recv, y_recv, diag_recv, line_recv):
    y, c, z, x = place()
    greet(pltpu.get_barrier_semaphore(), y, c, z, x)
    up, down = device_of(y, c, z + 1, x), device_of(y, c, z - 1, x)
    over_x, over_y = device_of(y, c, z, 1 - x), device_of(1 - y, c, z, x)
    twin = device_of(y, 1 - c, z, x)

    def block(quadrant, target_z, core):
        return block_of(*((1 - y) if quadrant >= 2 else y, core, target_z, (1 - x) if quadrant % 2 else x))

    def part(h):
        return pl.ds(h * half, half)

    def remote(src, dst, send_sem, recv_sem, target):
        return pltpu.make_async_remote_copy(
            src_ref=src, dst_ref=dst, send_sem=send_sem, recv_sem=recv_sem, device_id=target, device_id_type=MESH
        )

    def to_core(q, tz, h):
        return remote(
            in_ref.at[block(q, tz, 1 - c), part(h)],
            core_buf.at[q, tz, part(h)],
            core_sem.at[q, tz, h],
            core_recv.at[q, tz, h],
            twin,
        )

    def across(tz, h):
        return remote(
            core_buf.at[3, tz, part(h)],
            diag_buf.at[h, tz],
            (y_sem if h == 0 else x_sem).at[tz, 2],
            diag_recv.at[h, tz],
            over_y if h == 0 else over_x,
        )

    def to_x(tz, h):
        return remote(core_buf.at[1, tz, part(h)], x_buf.at[tz, part(h)], x_sem.at[tz, h], x_recv.at[tz, h], over_x)

    def to_y(tz, h):
        return remote(core_buf.at[2, tz, part(h)], y_buf.at[tz, part(h)], y_sem.at[tz, h], y_recv.at[tz, h], over_y)

    def along(way, tz):
        return remote(
            core_buf.at[0, tz], line_buf.at[way, tz], line_sem.at[way, tz], line_recv.at[way, tz],
            up if way == 0 else down,
        )

    def add_into(target, source):
        target[...] = (target[...].astype(jnp.float32) + source[...].astype(jnp.float32)).astype(target.dtype)

    def add_core(q, tz, h):
        to_core(q, tz, h).wait_recv()
        add_into(core_buf.at[q, tz, part(h)], in_ref.at[block(q, tz, c), part(h)])

    def through(tz):
        for h in range(2):
            add_core(3, tz, h)
            across(tz, h).start()
        add_core(1, tz, 1)
        to_x(tz, 1).start()
        add_core(2, tz, 0)
        to_y(tz, 0).start()
        add_core(1, tz, 0)
        across(tz, 0).wait_recv()
        add_into(core_buf.at[1, tz, part(0)], diag_buf.at[0, tz])
        to_x(tz, 0).start()
        add_core(2, tz, 1)
        across(tz, 1).wait_recv()
        add_into(core_buf.at[2, tz, part(1)], diag_buf.at[1, tz])
        to_y(tz, 1).start()
        for h in range(2):
            add_core(0, tz, h)

    def collect(tz):
        for h in (1, 0):
            to_x(tz, h).wait_recv()
            add_into(core_buf.at[0, tz, part(h)], x_buf.at[tz, part(h)])
        for h in (0, 1):
            to_y(tz, h).wait_recv()
            add_into(core_buf.at[0, tz, part(h)], y_buf.at[tz, part(h)])

    def by_distance(k, step):
        @pl.when(z + k < LINE)
        def _():
            step(z + k, 0)

        @pl.when(z >= k)
        def _():
            step(z - k, 1)

    def pass_on(tz, way):
        collect(tz)

        @pl.when((z > 0) if way == 0 else (z < LINE - 1))
        def _():
            along(way, tz).wait_recv()
            add_into(core_buf.at[0, tz], line_buf.at[way, tz])

        along(way, tz).start()

    for k in (3, 2, 1, 0):
        def offer(tz, way):
            for q in (3, 1, 2, 0):
                for h in ((1, 0) if q == 1 else (0, 1)):
                    to_core(q, tz, h).start()

        if k:
            by_distance(k, offer)
        else:
            offer(z, 0)
    by_distance(3, lambda tz, way: through(tz))
    by_distance(2, lambda tz, way: through(tz))
    by_distance(3, pass_on)
    by_distance(1, lambda tz, way: through(tz))
    by_distance(2, pass_on)
    through(z)
    by_distance(1, pass_on)
    collect(z)

    @pl.when(z > 0)
    def _():
        along(0, z).wait_recv()
        add_into(core_buf.at[0, z], line_buf.at[0, z])

    @pl.when(z < LINE - 1)
    def _():
        along(1, z).wait_recv()
        add_into(core_buf.at[0, z], line_buf.at[1, z])

    out_ref[...] = core_buf[0, z]
    for tz in range(LINE):
        for q in range(4):
            for h in range(2):
                to_core(q, tz, h).wait_send()
        for h in range(2):
            across(tz, h).wait_send()
            to_x(tz, h).wait_send()
            to_y(tz, h).wait_send()
    for k in (1, 2, 3):
        by_distance(k, lambda tz, way: along(way, tz).wait_send())


def scatter_sum(partial, collective_id):
    blocks, rows, width = partial.shape
    half = rows // 2
    dma = pltpu.SemaphoreType.DMA
    return pl.pallas_call(
        functools.partial(scatter_kernel, half),
        out_shape=jax.ShapeDtypeStruct((rows, width), partial.dtype),
        in_specs=[pl.BlockSpec(memory_space=pltpu.VMEM)],
        out_specs=pl.BlockSpec(memory_space=pltpu.VMEM),
        scratch_shapes=[
            pltpu.VMEM((4, LINE, rows, width), partial.dtype),
            pltpu.VMEM((LINE, rows, width), partial.dtype),
            pltpu.VMEM((LINE, rows, width), partial.dtype),
            pltpu.VMEM((2, LINE, half, width), partial.dtype),
            pltpu.VMEM((2, LINE, rows, width), partial.dtype),
            dma((4, LINE, 2)),
            dma((LINE, 3)),
            dma((LINE, 3)),
            dma((2, LINE)),
            dma((4, LINE, 2)),
            dma((LINE, 2)),
            dma((LINE, 2)),
            dma((2, LINE)),
            dma((2, LINE)),
        ],
        compiler_params=pltpu.CompilerParams(
            collective_id=collective_id, has_side_effects=True, vmem_limit_bytes=48 << 20
        ),
    )(partial)


def expert_kernel(plan, first_ref, rows_ref, gate_ref, up_ref, down_ref, out_ref, x_buf, weight_buf, sum_buf, result_buf):
    groups, tok_rows, top, capacity, reps, chunks, width = plan
    step = pl.program_id(0)
    group_rows = rows_ref.shape[0]
    seats = group_rows // tok_rows * capacity
    slots = reps * seats

    @pl.when(step < groups)
    def _():
        side = rows_ref[:, width:].astype(jnp.float32)
        row = lax.broadcasted_iota(jnp.int32, (group_rows, 1), 0)
        slot_iota = lax.broadcasted_iota(jnp.int32, (group_rows, slots), 1)
        pick = jnp.zeros((group_rows, slots), jnp.float32)
        upper, lower = pick, pick
        for k in range(top):
            replica = side[:, 2 * top + k : 2 * top + k + 1].astype(jnp.int32) - first_ref[0]
            slot = side[:, 3 * top + k : 3 * top + k + 1].astype(jnp.int32)
            here = (replica >= 0) & (replica < reps) & (slot < capacity)
            seat = jnp.where(here, replica * seats + row // tok_rows * capacity + slot, -1)
            hit = seat == slot_iota
            pick = jnp.where(hit, 1.0, pick)
            upper = jnp.where(hit, side[:, k : k + 1], upper)
            lower = jnp.where(hit, side[:, top + k : top + k + 1], lower)
        picked = jnp.dot(
            pick.T.astype(jnp.bfloat16), rows_ref[:, :width], preferred_element_type=jnp.float32
        ).astype(jnp.bfloat16)
        for j in range(reps):
            x_buf[j, pl.ds(step * seats, seats)] = picked[j * seats : (j + 1) * seats]
        weight_buf[step, :, :slots] = upper.astype(jnp.bfloat16)
        weight_buf[step, :, slots:] = lower.astype(jnp.bfloat16)

    turn = step - groups

    @pl.when((turn >= 0) & (turn < reps * chunks))
    def _():
        j, chunk = turn // chunks, turn % chunks
        expert_in = x_buf[j]
        gate = jnp.dot(expert_in, gate_ref[0], preferred_element_type=jnp.float32)
        raised = jnp.dot(expert_in, up_ref[0], preferred_element_type=jnp.float32)
        hidden = (gate / (1.0 + jnp.exp(-gate)) * raised).astype(jnp.bfloat16)
        part = jnp.dot(hidden, down_ref[0], preferred_element_type=jnp.float32)

        @pl.when(chunk == 0)
        def _():
            sum_buf[...] = part

        @pl.when(chunk > 0)
        def _():
            sum_buf[...] += part

        @pl.when(chunk == chunks - 1)
        def _():
            for g in range(groups):
                result = sum_buf[g * seats : (g + 1) * seats].astype(jnp.bfloat16)
                result_buf[g, pl.ds(j * seats, seats)] = result
                result_buf[g, pl.ds(slots + j * seats, seats)] = result

    group = turn - reps * chunks

    @pl.when(group >= 0)
    def _():
        out_ref[...] = jnp.dot(
            weight_buf[group], result_buf[group], preferred_element_type=jnp.float32
        ).astype(out_ref.dtype)


def run_experts(first, rows, up_gate, down, tok_rows, top, capacity):
    row_total, padded = rows.shape
    reps, hidden_units, width = down.shape
    group_rows, chunks = 4 * tok_rows, 2
    groups = row_total // group_rows
    piece = hidden_units // chunks
    seats = 4 * capacity
    slots = reps * seats
    turns = reps * chunks

    def turn_of(step):
        return jnp.clip(step - groups, 0, turns - 1)

    return pl.pallas_call(
        functools.partial(expert_kernel, (groups, tok_rows, top, capacity, reps, chunks, width)),
        grid=(2 * groups + turns,),
        out_shape=jax.ShapeDtypeStruct((row_total, width), jnp.bfloat16),
        in_specs=[
            pl.BlockSpec(memory_space=pltpu.SMEM),
            pl.BlockSpec((group_rows, padded), lambda s: (jnp.minimum(s, groups - 1), 0)),
            pl.BlockSpec((1, width, piece), lambda s: (turn_of(s) // chunks, 0, turn_of(s) % chunks)),
            pl.BlockSpec((1, width, piece), lambda s: (turn_of(s) // chunks, 0, chunks + turn_of(s) % chunks)),
            pl.BlockSpec((1, piece, width), lambda s: (turn_of(s) // chunks, turn_of(s) % chunks, 0)),
        ],
        out_specs=pl.BlockSpec((group_rows, width), lambda s: (jnp.maximum(s - groups - turns, 0), 0)),
        scratch_shapes=[
            pltpu.VMEM((reps, groups * seats, width), jnp.bfloat16),
            pltpu.VMEM((groups, group_rows, 2 * slots), jnp.bfloat16),
            pltpu.VMEM((groups * seats, width), jnp.float32),
            pltpu.VMEM((groups, 2 * slots, width), jnp.bfloat16),
        ],
        compiler_params=pltpu.CompilerParams(
            dimension_semantics=("arbitrary",), vmem_limit_bytes=52 << 20
        ),
    )(first, rows, up_gate, up_gate, down)


SIDE = 128


def per_device_gathered(
    hidden_in,
    context,
    out_proj,
    norm_gain,
    router,
    expert_ids,
    replica_expert,
    split_pick,
    up_gate,
    down,
):
    tok_rows, model_width = hidden_in.shape
    expert_total = router.shape[1]
    top_count = expert_ids.shape[1]
    replica_total = replica_expert.shape[0]
    local_reps = up_gate.shape[0]
    blocks = lax.axis_size("dp") * lax.axis_size("expert")
    me = lax.axis_index("dp") * lax.axis_size("expert") + lax.axis_index("expert")
    capacity = max(2, 2 * tok_rows * top_count // replica_total)
    side = jnp.pad(router, ((0, 0), (0, SIDE - expert_total)))
    proj_rows = gather_rows(jnp.concatenate([out_proj, side], axis=1), 0)
    proj_rows = proj_rows.reshape(blocks * out_proj.shape[0], model_width + SIDE)
    router_rows = proj_rows[:, model_width : model_width + expert_total]
    replica, slot_index = route_block(expert_ids, split_pick, replica_expert)
    slot_index = jnp.minimum(slot_index, capacity)
    summed = jnp.dot(context, proj_rows, preferred_element_type=jnp.float32)[:, :model_width]
    residual = hidden_in.astype(jnp.float32) + summed
    normed = rms_norm(residual, norm_gain)
    logits = jnp.dot(normed, router_rows, preferred_element_type=jnp.float32)
    hit_mask = expert_ids[:, :, None] == lax.iota(jnp.int32, expert_total)[None, None, :]
    chosen = jnp.sum(jnp.where(hit_mask, logits[:, None, :], 0.0), axis=-1)
    raised = jnp.exp(chosen)
    route_weight = raised / jnp.sum(raised, axis=-1, keepdims=True)
    upper = route_weight.astype(jnp.bfloat16)
    lower = (route_weight - upper.astype(jnp.float32)).astype(jnp.bfloat16)
    side = jnp.concatenate(
        [upper, lower, replica.astype(jnp.bfloat16), slot_index.astype(jnp.bfloat16)], axis=1
    )
    side = jnp.pad(side, ((0, 0), (0, SIDE - 4 * top_count)))
    all_rows = gather_rows(jnp.concatenate([normed, side], axis=1), 1)
    first = jnp.full((1,), me * local_reps, jnp.int32)
    partial = run_experts(
        first,
        all_rows.reshape(blocks * tok_rows, model_width + SIDE),
        up_gate,
        down,
        tok_rows,
        top_count,
        capacity,
    ).reshape(blocks, tok_rows, model_width)
    combined = scatter_sum(partial, 2)
    return (residual + combined.astype(jnp.float32)).astype(jnp.bfloat16)


def solution(mesh):
    plan = per_device_gathered if (mesh.shape["dp"], mesh.shape["expert"]) == (4, 8) else per_device
    return jax.shard_map(
        plan,
        mesh=mesh,
        in_specs=(
            P(("dp", "expert"), None),
            P(("dp", "expert"), None),
            P(("dp", "expert"), None),
            P(),
            P(("dp", "expert"), None),
            P(("dp", "expert"), None),
            P(),
            P(("dp", "expert"), None),
            P(("dp", "expert"), None, None),
            P(("dp", "expert"), None, None),
        ),
        out_specs=P(("dp", "expert"), None),
        check_vma=False,
    )
```
